32 devices in a mesh: tm: 4 (over z), space: 8 (over y, x, core).
Axes of the slice: x: 2, y: 2, z: 4, core: 2. Of those that a mesh axis runs over, the one named last changes fastest.
Arguments:
- frames: bfloat16 [4, 96, 32, 1280], P('tm', None, 'space'), may hold values from -6 to 6
- cache: bfloat16 [2, 96, 32, 1280], P(None, 'tm', 'space'), may hold values from -6 to 6
- grad_out: bfloat16 [4, 96, 32, 1280], P('tm', None, 'space'), may hold values from -6 to 6
- weight: bfloat16 [3, 3, 3, 96, 96], replicated, may hold values from -0.125 to 0.125
Outputs:
- input_grad: bfloat16 [4, 96, 32, 1280], P('tm', None, 'space')
- cache_grad: bfloat16 [2, 96, 32, 1280], P(None, 'tm', 'space')
- weight_grad: float32 [3, 3, 3, 96, 96], replicated
The draws below stay inside these ranges and needn't reach their ends.
All inputs are finite; a program needn't handle non-finite values.
Results may differ from the reference program's by a relative error of at most 0.0041.
Values may be sent and summed in bfloat16 or wider, within the bound.
A program may use at most 64 MiB of HBM per device.

```python
import math
import jax
import jax.numpy as jnp
from jax import lax

C = 96
WIDTH = 1280
FRAMES = 4
HEIGHT = 32


def level_of(key, dims, shards, least, largest):
    loudness = 1.0
    for dim, blocks in shards:
        steps = jax.random.uniform(jax.random.fold_in(jax.random.fold_in(key, 6), dim), (blocks,), jnp.float32, least / len(shards), largest / len(shards))
        loudness = loudness * jnp.repeat(jnp.exp(steps), dims[dim] // blocks).reshape((-1,) + (1,) * (len(dims) - 1 - dim))
    return loudness


def centred(own_key, dims, spread, most, cuts=(), kind=jnp.bfloat16):
    array = jax.random.normal(own_key, dims, jnp.float32) * spread
    if len(cuts) > 0:
        array = level_of(own_key, dims, cuts, -0.22, 0.18) * array
    return jnp.clip(array, min=-most, max=most).astype(kind)


def setup_inputs(seed: int = 0) -> dict:
    key_of = jax.random.split(jax.random.key(seed), 5)
    return {
        "frames": centred(key_of[0], (FRAMES, C, HEIGHT, WIDTH), 1.0, 6.0, ((0, 4), (2, 8))),
        "cache": centred(key_of[1], (2, C, HEIGHT, WIDTH), 1.0, 6.0, ((1, 4), (2, 8))),
        "grad_out": centred(key_of[2], (FRAMES, C, HEIGHT, WIDTH), 1.0, 6.0, ((0, 4), (2, 8))),
        "weight": centred(key_of[3], (3, 3, 3, C, C), (27 * C) ** -0.5, 0.125),
    }


def rounded(value):
    return lax.optimization_barrier(value.astype(jnp.bfloat16)).astype(jnp.float32)

def reference(frames, cache, grad_out, weight):
    extended = jnp.concatenate([cache, frames], axis=0)
    padded_in = jnp.pad(extended, ((0, 0), (0, 0), (1, 1), (1, 1)))
    padded_out = jnp.pad(grad_out, ((0, 0), (0, 0), (1, 1), (1, 1)))
    weight_full = weight.astype(jnp.float32)
    band = math.gcd(HEIGHT, 16)
    band_count = HEIGHT // band

    def one_band(band_index):
        start = (band_index * band).astype(jnp.int32)
        band_in = lax.dynamic_slice_in_dim(padded_in, start, band + 2, 2)
        band_out = lax.dynamic_slice_in_dim(padded_out, start, band + 2, 2)
        weight_sum = jnp.zeros((3, 3, 3, C, C), jnp.float32)
        terms = []
        for frame_index in range(FRAMES):
            accum = jnp.zeros((3, C, band, WIDTH), jnp.float32)
            grad_full = band_out[frame_index, :, 1:1 + band, 1:1 + WIDTH].astype(jnp.float32)
            for row_tap in range(3):
                for col_tap in range(3):
                    window = band_out[frame_index, :, 2 - row_tap:2 - row_tap + band, 2 - col_tap:2 - col_tap + WIDTH].astype(jnp.float32)
                    accum = accum + jnp.einsum('koc,ohw->kchw', weight_full[:, row_tap, col_tap], window, precision=lax.Precision.HIGHEST)
                    inputs = band_in[frame_index:frame_index + 3, :, row_tap:row_tap + band, col_tap:col_tap + WIDTH].astype(jnp.float32)
                    contrib = jnp.einsum('ohw,kchw->koc', grad_full, inputs, precision=lax.Precision.HIGHEST)
                    weight_sum = weight_sum.at[:, row_tap, col_tap].add(contrib)
            terms.append(accum)
        grads = []
        for frame_index in range(FRAMES):
            total = terms[frame_index][2]
            if frame_index + 1 < FRAMES:
                total = total + rounded(terms[frame_index + 1][1])
            if frame_index + 2 < FRAMES:
                total = total + rounded(terms[frame_index + 2][0])
            grads.append(total.astype(jnp.bfloat16))
        input_band = jnp.stack(grads, axis=0)
        cache_first = terms[0][0]
        cache_second = terms[0][1] + rounded(terms[1][0])
        cache_band = jnp.stack([cache_first, cache_second], axis=0).astype(jnp.bfloat16)
        return (input_band, cache_band, weight_sum)
    input_bands, cache_bands, weight_parts = lax.map(one_band, jnp.arange(band_count, dtype=jnp.int32))
    input_grad = jnp.transpose(input_bands, (1, 2, 0, 3, 4)).reshape(FRAMES, C, HEIGHT, WIDTH)
    cache_grad = jnp.transpose(cache_bands, (1, 2, 0, 3, 4)).reshape(2, C, HEIGHT, WIDTH)
    scale = 1.0 / math.sqrt(FRAMES * HEIGHT * WIDTH)
    weight_grad = lax.optimization_barrier(jnp.sum(weight_parts, axis=0)) * scale
    return (input_grad, cache_grad, weight_grad)
```

```python
import functools
import math

import jax
import jax.numpy as jnp
from jax import lax
from jax.experimental import pallas as pl
from jax.experimental.pallas import tpu as pltpu
from jax.sharding import PartitionSpec as P

MESH = pl.DeviceIdType.MESH
OWN, N1, N2, C1, C0 = range(5)
TO_PREV, FWD_PREV, TO_NEXT, FWD_C1, FWD_C0 = range(5)


def kernel(
    nz, ns, chunks, channels, share, scale,
    g_ref, xs_ref, wl_ref, out_ref, wg_a_ref, wg_b_ref,
    gp, sc, dacc, wtmp, acc_a, acc_b,
    sb_a, rb_a, zs_a, zb_a, gb_a, sb_b, rb_b, zs_b, zb_b, gb_b,
    z_send, z_recv, h_send, h_recv,
    rs_send, rs_recv, zz_send, zz_recv, ag_send, ag_recv,
):
    j = lax.axis_index("tm")
    s = lax.axis_index("space")
    rows, _, cols = g_ref.shape
    k_row = 3 * channels
    taps = 3 * k_row
    last = nz - 1

    barrier = pltpu.get_barrier_semaphore()
    for k in range(1, ns):
        pl.semaphore_signal(barrier, inc=1, device_id={"space": lax.rem(s + k, ns)}, device_id_type=MESH)
    for k in range(1, nz):
        pl.semaphore_signal(barrier, inc=1, device_id={"tm": lax.rem(j + k, nz)}, device_id_type=MESH)
    pl.semaphore_wait(barrier, ns - 1 + nz - 1)

    def row_copy(stream, slot_from, slot_to, r, target):
        src = g_ref.at[r] if slot_from == OWN else gp.at[slot_from, r + 1]
        return pltpu.make_async_remote_copy(
            src_ref=src, dst_ref=gp.at[slot_to, r + 1],
            send_sem=z_send.at[stream, r], recv_sem=z_recv.at[slot_to, r],
            device_id={"tm": target}, device_id_type=MESH)

    prev = lax.rem(j + nz - 1, nz)
    nxt = lax.rem(j + 1, nz)

    def to_prev(r):
        return row_copy(TO_PREV, OWN, N1, r, prev)

    def fwd_prev(r):
        return row_copy(FWD_PREV, N1, N2, r, prev)

    def own_c0(r):
        return row_copy(TO_NEXT, OWN, C0, r, nxt)

    def own_c1(r):
        return row_copy(TO_NEXT, OWN, C1, r, nxt)

    def fwd_c1(r):
        return row_copy(FWD_C1, C1, C1, r, nxt)

    def fwd_c0(r):
        return row_copy(FWD_C0, C0, C0, r, nxt)

    for r in range(rows):
        pl.when(j >= 1)(lambda: to_prev(r).start())
        pl.when(j == 0)(lambda: own_c0(r).start())
        if nz > 2:
            pl.when(j == 1)(lambda: own_c1(r).start())

    def halo_up(slot):
        src = g_ref.at[0] if slot == OWN else gp.at[slot, 1]
        return pltpu.make_async_remote_copy(
            src_ref=src, dst_ref=gp.at[slot, rows + 1],
            send_sem=h_send.at[slot, 0], recv_sem=h_recv.at[slot, 0],
            device_id={"space": lax.rem(s + ns - 1, ns)}, device_id_type=MESH)

    def halo_down(slot):
        src = g_ref.at[rows - 1] if slot == OWN else gp.at[slot, rows]
        return pltpu.make_async_remote_copy(
            src_ref=src, dst_ref=gp.at[slot, 0],
            send_sem=h_send.at[slot, 1], recv_sem=h_recv.at[slot, 1],
            device_id={"space": lax.rem(s + 1, ns)}, device_id_type=MESH)

    def halo_start_up(slot):
        pl.when(s >= 1)(lambda: halo_up(slot).start())

    def halo_start_down(slot):
        pl.when(s < ns - 1)(lambda: halo_down(slot).start())

    def halo_wait(slot):
        @pl.when(s >= 1)
        def _():
            halo_up(slot).wait_send()
            halo_down(slot).wait_recv()

        @pl.when(s < ns - 1)
        def _():
            halo_down(slot).wait_send()
            halo_up(slot).wait_recv()

    halo_start_up(OWN)
    halo_start_down(OWN)

    @pl.when(s == 0)
    def _():
        for slot in range(5):
            gp[slot, 0] = jnp.zeros(gp.shape[2:], gp.dtype)

    @pl.when(s == ns - 1)
    def _():
        for slot in range(5):
            gp[slot, rows + 1] = jnp.zeros(gp.shape[2:], gp.dtype)

    dacc[...] = jnp.zeros_like(dacc)
    acc_a[...] = jnp.zeros_like(acc_a)
    acc_b[...] = jnp.zeros_like(acc_b)
    wtmp[...] = jnp.zeros_like(wtmp)
    for r in range(rows):
        gp[OWN, r + 1] = g_ref[r]

    lane = lax.broadcasted_iota(jnp.int32, (channels, cols), 1)
    tile = 256 if cols % 256 == 0 else 128
    tiles = cols // tile
    stack = xs_ref.shape[1]
    wide = 128
    wlane = lax.broadcasted_iota(jnp.int32, (taps, wide), 1)

    def shift_row(slot, p):
        value = gp[slot, p]
        full = value.astype(jnp.float32)
        ahead = jnp.where(lane == cols - 1, 0.0, pltpu.roll(full, cols - 1, 1))
        behind = jnp.where(lane == 0, 0.0, pltpu.roll(full, 1, 1))
        base = pl.multiple_of(p * k_row, 16)
        sc[pl.ds(base, channels), :] = ahead.astype(jnp.bfloat16)
        sc[pl.ds(pl.multiple_of(base + channels, 16), channels), :] = value
        sc[pl.ds(pl.multiple_of(base + 2 * channels, 16), channels), :] = behind.astype(jnp.bfloat16)

    def compute_row(slot, h, first):
        base = pl.multiple_of(h * k_row, 16)

        def col_step(i, carry):
            at = pl.multiple_of(i * tile, tile)
            block = sc[pl.ds(base, taps), pl.ds(at, tile)]
            dacc[h, :, pl.ds(at, tile)] += jnp.dot(
                wl_ref[slot], block, preferred_element_type=jnp.float32)
            part = lax.dot_general(
                block, xs_ref[h, :, pl.ds(at, tile)], (((1,), (1,)), ((), ())),
                preferred_element_type=jnp.float32)
            wtmp[:, :stack] += part
            return carry

        lax.fori_loop(0, tiles, col_step, 0)

    def placed_cache(block, shift_from):
        turned = pltpu.roll(block, lax.rem(j * share + 2 * wide - shift_from, wide), 1)
        inside = jnp.logical_and(wlane >= j * share, wlane < (j + 1) * share)
        return jnp.where(inside, turned, 0.0)

    def process(slot, hook=None):
        def do_shift(p, carry):
            shift_row(slot, p)
            return carry

        lax.fori_loop(0, rows + 2, do_shift, 0)
        if hook is None:
            def do_row(h, carry):
                compute_row(slot, h, False)
                return carry

            lax.fori_loop(0, rows, do_row, 0)
        else:
            for h in range(rows):
                hook(h)
                compute_row(slot, h, False)
        low = wtmp[:, :wide]
        x_part = jnp.where(wlane < channels, low, 0.0)
        if slot == OWN:
            acc_a[:taps, :] += x_part
        if slot == N1:
            acc_b[:taps, :] += x_part
        if slot == N2:
            acc_b[taps:2 * taps, :] += x_part

        def as_g0():
            acc_b[taps:2 * taps, :] += placed_cache(wtmp[:, :wide], channels)
            acc_b[:taps, :] += placed_cache(wtmp[:, wide:], 0)

        def as_g1():
            acc_b[taps:2 * taps, :] += placed_cache(wtmp[:, wide:], 0)

        if slot == OWN:
            pl.when(j == 0)(as_g0)
            pl.when(j == 1)(as_g1)
        if slot == N1:
            pl.when(j == 0)(as_g1)
        if slot == C1:
            as_g1()
        if slot == C0:
            as_g0()
        wtmp[...] = jnp.zeros_like(wtmp)

    def reduction(index, acc, sb, rb, zs, zb, gb, out, ck):
        def rs_copy(k):
            to = lax.rem(s + k, ns)
            return pltpu.make_async_remote_copy(
                src_ref=sb.at[to], dst_ref=rb.at[s],
                send_sem=rs_send.at[index, k], recv_sem=rs_recv.at[index, s],
                device_id={"space": to}, device_id_type=MESH)

        def rs_landed(k):
            source = lax.rem(s + ns - k, ns)
            return pltpu.make_async_remote_copy(
                src_ref=sb.at[source], dst_ref=rb.at[source],
                send_sem=rs_send.at[index, k], recv_sem=rs_recv.at[index, source],
                device_id={"space": source}, device_id_type=MESH)

        def z_copy(k):
            return pltpu.make_async_remote_copy(
                src_ref=zs, dst_ref=zb.at[j],
                send_sem=zz_send.at[index, k], recv_sem=zz_recv.at[index, j],
                device_id={"tm": lax.rem(j + k, nz)}, device_id_type=MESH)

        def z_landed(k):
            source = lax.rem(j + nz - k, nz)
            return pltpu.make_async_remote_copy(
                src_ref=zs, dst_ref=zb.at[source],
                send_sem=zz_send.at[index, k], recv_sem=zz_recv.at[index, source],
                device_id={"tm": source}, device_id_type=MESH)

        def ag_copy(k):
            return pltpu.make_async_remote_copy(
                src_ref=gb.at[s], dst_ref=gb.at[s],
                send_sem=ag_send.at[index, k], recv_sem=ag_recv.at[index, s],
                device_id={"space": lax.rem(s + k, ns)}, device_id_type=MESH)

        def ag_landed(k):
            source = lax.rem(s + ns - k, ns)
            return pltpu.make_async_remote_copy(
                src_ref=gb.at[source], dst_ref=gb.at[source],
                send_sem=ag_send.at[index, k], recv_sem=ag_recv.at[index, source],
                device_id={"space": source}, device_id_type=MESH)

        def scatter():
            for q in range(ns):
                sb[q] = acc[q * ck:(q + 1) * ck, :].astype(jnp.bfloat16)
            for k in range(1, ns):
                rs_copy(k).start()

        def across():
            total = acc[pl.ds(pl.multiple_of(s * ck, 16), ck), :]
            for k in range(1, ns):
                rs_landed(k).wait_recv()
                total = total + rb[lax.rem(s + ns - k, ns)].astype(jnp.float32)
            zs[...] = total
            for k in range(1, nz):
                z_copy(k).start()

        def gather():
            zb[j] = zs[...]
            for k in range(1, nz):
                z_landed(k).wait_recv()
            total = zb[0]
            for q in range(1, nz):
                total = total + zb[q]
            gb[s] = (total * scale).astype(jnp.bfloat16)
            for k in range(1, ns):
                ag_copy(k).start()

        def finish():
            for k in range(1, ns):
                ag_landed(k).wait_recv()
            for q in range(ns):
                out[q * ck:(q + 1) * ck, :] = gb[q].astype(jnp.float32)
            for k in range(1, ns):
                rs_copy(k).wait_send()
                ag_copy(k).wait_send()
            for k in range(1, nz):
                z_copy(k).wait_send()

        return scatter, across, gather, finish

    a_steps = reduction(0, acc_a, sb_a, rb_a, zs_a, zb_a, gb_a, wg_a_ref, chunks[0])
    b_steps = reduction(1, acc_b, sb_b, rb_b, zs_b, zb_b, gb_b, wg_b_ref, chunks[1])

    halo_wait(OWN)
    process(OWN)
    a_steps[0]()

    has_n1 = j < last
    has_n2 = j < last - 1
    for r in range(rows):
        @pl.when(has_n1)
        def _():
            to_prev(r).wait_recv()
            pl.when(j >= 1)(lambda: fwd_prev(r).start())
            if r == 0:
                halo_start_up(N1)
            if r == rows - 1:
                halo_start_down(N1)

        @pl.when(j == 1)
        def _():
            own_c0(r).wait_recv()
            if nz > 2:
                fwd_c0(r).start()
            if r == 0:
                halo_start_up(C0)
            if r == rows - 1:
                halo_start_down(C0)

        if nz > 2:
            @pl.when(j >= 2)
            def _():
                own_c1(r).wait_recv()
                pl.when(j < last)(lambda: fwd_c1(r).start())
                if r == 0:
                    halo_start_up(C1)
                if r == rows - 1:
                    halo_start_down(C1)

    @pl.when(has_n1)
    def _():
        halo_wait(N1)
        process(N1)

    a_steps[1]()

    def c0_row(r):
        own_c0(r).wait_recv()
        pl.when(j < last)(lambda: fwd_c0(r).start())
        if r == 0:
            halo_start_up(C0)
        if r == rows - 1:
            halo_start_down(C0)

    if nz > 2:
        @pl.when(j >= 2)
        def _():
            halo_wait(C1)
            process(C1, c0_row)

    @pl.when(j >= 1)
    def _():
        halo_wait(C0)
        process(C0)

    a_steps[2]()

    if nz > 2:
        @pl.when(has_n2)
        def _():
            for r in range(rows):
                fwd_prev(r).wait_recv()
                if r == 0:
                    halo_start_up(N2)
                if r == rows - 1:
                    halo_start_down(N2)
            halo_wait(N2)
            process(N2)

    b_steps[0]()
    out_ref[...] = dacc[...].astype(jnp.bfloat16)
    a_steps[3]()
    b_steps[1]()
    b_steps[2]()

    for r in range(rows):
        @pl.when(j >= 1)
        def _():
            to_prev(r).wait_send()

        @pl.when(jnp.logical_and(j >= 1, has_n1))
        def _():
            fwd_prev(r).wait_send()

        @pl.when(j == 0)
        def _():
            own_c0(r).wait_send()

        if nz > 2:
            @pl.when(j == 1)
            def _():
                own_c1(r).wait_send()

            @pl.when(jnp.logical_and(j >= 1, j < last))
            def _():
                fwd_c0(r).wait_send()

            @pl.when(jnp.logical_and(j >= 2, j < last))
            def _():
                fwd_c1(r).wait_send()
    b_steps[3]()


def up_to(value, step):
    return -(-value // step) * step


def per_device(nz, ns, frames, cache, grad_out, weight):
    j = lax.axis_index("tm")
    _, channels, rows, cols = frames.shape
    share = cache.shape[1]
    taps = 9 * channels
    gap = up_to(share, 32) - share
    lead = 128 - channels
    stack = 128 + up_to(share, 32)
    g = jnp.transpose(grad_out[0], (1, 0, 2))

    def stacked(x_rows, first, second, dim):
        def empty(like, count):
            shape = list(like.shape)
            shape[dim] = count
            return jnp.zeros(shape, like.dtype)

        parts = [x_rows, first]
        if lead > share:
            parts.append(empty(first, lead - share))
        parts.append(second)
        if gap:
            parts.append(empty(second, gap))
        return jnp.concatenate(parts, axis=dim)

    xs = stacked(
        jnp.transpose(frames[0], (1, 0, 2)), jnp.transpose(cache[0], (1, 0, 2)),
        jnp.transpose(cache[1], (1, 0, 2)), 1)
    wt = jnp.transpose(weight[:, ::-1], (0, 4, 1, 2, 3)).reshape(3, channels, taps)
    wc = lax.dynamic_slice_in_dim(wt, j * share, share, axis=1)
    zx = jnp.zeros_like(wt[0])
    zc = jnp.zeros_like(wc[0])

    def pick(is_g0, is_g1):
        first = jnp.where(is_g0, wc[0], zc)
        second = jnp.where(is_g0, wc[1], jnp.where(is_g1, wc[0], zc))
        return first, second

    no = jnp.zeros((), bool)
    wl = jnp.stack([
        stacked(wt[2], *pick(j == 0, j == 1), 0),
        stacked(wt[1], *pick(no, j == 0), 0),
        stacked(wt[0], zc, zc, 0),
        stacked(zx, zc, wc[0], 0),
        stacked(zx, wc[0], wc[1], 0),
    ])
    chunks = (up_to(-(-taps // ns), 16), up_to(-(-2 * taps // ns), 16))
    scale = 1.0 / math.sqrt(nz * ns * rows * cols)
    f32, bf16 = jnp.float32, jnp.bfloat16

    def buffers(ck):
        return [
            pltpu.VMEM((ns, ck, 128), bf16), pltpu.VMEM((ns, ck, 128), bf16),
            pltpu.VMEM((ck, 128), f32), pltpu.VMEM((nz, ck, 128), f32),
            pltpu.VMEM((ns, ck, 128), bf16)]

    vmem = pl.BlockSpec(memory_space=pltpu.VMEM)
    dma = pltpu.SemaphoreType.DMA
    out, wg_a, wg_b = pl.pallas_call(
        functools.partial(kernel, nz, ns, chunks, channels, share, scale),
        out_shape=(
            jax.ShapeDtypeStruct((rows, stack, cols), bf16),
            jax.ShapeDtypeStruct((ns * chunks[0], 128), f32),
            jax.ShapeDtypeStruct((ns * chunks[1], 128), f32),
        ),
        in_specs=[vmem] * 3,
        out_specs=(vmem,) * 3,
        scratch_shapes=[
            pltpu.VMEM((5, rows + 2, channels, cols), bf16),
            pltpu.VMEM(((rows + 2) * 3 * channels, cols), bf16),
            pltpu.VMEM((rows, stack, cols), f32),
            pltpu.VMEM((taps, 256), f32),
            pltpu.VMEM((ns * chunks[0], 128), f32),
            pltpu.VMEM((ns * chunks[1], 128), f32),
            *buffers(chunks[0]), *buffers(chunks[1]),
            dma((5, rows)), dma((5, rows)), dma((5, 2)), dma((5, 2)),
            dma((2, ns)), dma((2, ns)), dma((2, nz)), dma((2, nz)), dma((2, ns)), dma((2, ns)),
        ],
        compiler_params=pltpu.CompilerParams(
            collective_id=0, has_side_effects=True, vmem_limit_bytes=60 * 1024 * 1024),
    )(g, xs, wl)
    input_grad = jnp.transpose(out[:, :channels], (1, 0, 2))[None]
    cache_grad = jnp.stack([
        jnp.transpose(out[:, channels:channels + share], (1, 0, 2)),
        jnp.transpose(out[:, 128:128 + share], (1, 0, 2))])

    def unpacked(rows_of, count):
        cut = rows_of[:count * taps, :channels].reshape(count, 3, 3, channels, channels)
        return cut[:, ::-1]

    low = unpacked(wg_b, 2)
    weight_grad = jnp.concatenate([low[1:], low[:1], unpacked(wg_a, 1)], axis=0)
    return (input_grad, cache_grad, weight_grad)


def solution(mesh):
    placed = (
        P("tm", None, "space", None),
        P(None, "tm", "space", None),
        P("tm", None, "space", None),
        P(),
    )
    return jax.shard_map(
        functools.partial(per_device, mesh.shape["tm"], mesh.shape["space"]),
        mesh=mesh,
        in_specs=placed,
        out_specs=(P("tm", None, "space", None), P(None, "tm", "space", None), P()),
        check_vma=False,
    )
```

```python
import functools
import math

import jax
import jax.numpy as jnp
from jax import lax
from jax.experimental import pallas as pl
from jax.experimental.pallas import tpu as pltpu
from jax.sharding import PartitionSpec as P

MESH = pl.DeviceIdType.MESH
OWN, N1, N2, C1, C0 = range(5)
TO_PREV, FWD_PREV, TO_NEXT, FWD_C1, FWD_C0 = range(5)


def kernel(
    nz, ns, ck, channels, share, scale,
    g_ref, x_ref, c_ref, wt_ref, wc_ref, ig_ref, cg_ref, wg_ref,
    gp, sc, dacc, wtmp, acc, xs_ref, wl_ref,
    sb, rb, zs, zb, gb,
    z_send, z_recv, h_send, h_recv,
    rs_send, rs_recv, zz_send, zz_recv, ag_send, ag_recv,
):
    assert nz == 4
    j = lax.axis_index("tm")
    s = lax.axis_index("space")
    rows, _, cols = g_ref.shape
    k_row = 3 * channels
    taps = 3 * k_row
    last = nz - 1
    order = [0, rows - 1, *range(1, rows - 1)]
    high = 128
    late = jnp.where(j < last - 1, N2, C1)

    barrier = pltpu.get_barrier_semaphore()
    for k in range(1, ns):
        pl.semaphore_signal(barrier, inc=1, device_id={"space": lax.rem(s + k, ns)}, device_id_type=MESH)
    for k in range(1, nz):
        pl.semaphore_signal(barrier, inc=1, device_id={"tm": lax.rem(j + k, nz)}, device_id_type=MESH)
    pl.semaphore_wait(barrier, ns - 1 + nz - 1)

    def row_copy(stream, slot_from, slot_to, r, target):
        src = g_ref.at[r] if slot_from == OWN else gp.at[slot_from, r + 1]
        return pltpu.make_async_remote_copy(
            src_ref=src, dst_ref=gp.at[slot_to, r + 1],
            send_sem=z_send.at[stream, r], recv_sem=z_recv.at[slot_to, r],
            device_id={"tm": target}, device_id_type=MESH)

    prev = lax.rem(j + nz - 1, nz)
    nxt = lax.rem(j + 1, nz)

    def to_prev(r):
        return row_copy(TO_PREV, OWN, N1, r, prev)

    def fwd_prev(r):
        return row_copy(FWD_PREV, N1, N2, r, prev)

    def own_c0(r):
        return row_copy(TO_NEXT, OWN, C0, r, nxt)

    def own_c1(r):
        return row_copy(TO_NEXT, OWN, C1, r, nxt)

    def fwd_c1(r):
        return row_copy(FWD_C1, C1, C1, r, nxt)

    def fwd_c0(r):
        return row_copy(FWD_C0, C0, C0, r, nxt)

    for r in order:
        pl.when(j >= 1)(lambda: to_prev(r).start())
        pl.when(j == 0)(lambda: own_c0(r).start())
    pl.when(j == 1)(lambda: own_c1(order[0]).start())

    def halo_up(slot):
        src = g_ref.at[0] if slot is OWN else gp.at[slot, 1]
        return pltpu.make_async_remote_copy(
            src_ref=src, dst_ref=gp.at[slot, rows + 1],
            send_sem=h_send.at[slot, 0], recv_sem=h_recv.at[slot, 0],
            device_id={"space": lax.rem(s + ns - 1, ns)}, device_id_type=MESH)

    def halo_down(slot):
        src = g_ref.at[rows - 1] if slot is OWN else gp.at[slot, rows]
        return pltpu.make_async_remote_copy(
            src_ref=src, dst_ref=gp.at[slot, 0],
            send_sem=h_send.at[slot, 1], recv_sem=h_recv.at[slot, 1],
            device_id={"space": lax.rem(s + 1, ns)}, device_id_type=MESH)

    def halo_start_up(slot):
        pl.when(s >= 1)(lambda: halo_up(slot).start())

    def halo_start_down(slot):
        pl.when(s < ns - 1)(lambda: halo_down(slot).start())

    def halo_wait(slot):
        @pl.when(s >= 1)
        def _():
            halo_up(slot).wait_send()
            halo_down(slot).wait_recv()

        @pl.when(s < ns - 1)
        def _():
            halo_down(slot).wait_send()
            halo_up(slot).wait_recv()

    halo_start_up(OWN)
    halo_start_down(OWN)

    @pl.when(s == 0)
    def _():
        for slot in range(5):
            gp[slot, 0] = jnp.zeros(gp.shape[2:], gp.dtype)

    @pl.when(s == ns - 1)
    def _():
        for slot in range(5):
            gp[slot, rows + 1] = jnp.zeros(gp.shape[2:], gp.dtype)

    for r in range(rows):
        gp[OWN, r + 1] = g_ref[r]
    wtmp[...] = jnp.zeros_like(wtmp)
    acc[...] = jnp.zeros_like(acc)
    stack = xs_ref.shape[1]
    xs_ref[:, channels:, :] = jnp.zeros((rows, stack - channels, cols), xs_ref.dtype)
    wl_ref[:, channels:, :] = jnp.zeros((5, stack - channels, taps), wl_ref.dtype)
    for h in range(rows):
        xs_ref[h, :channels, :] = x_ref[h]
        xs_ref[h, channels:channels + share, :] = c_ref[0, h]
        xs_ref[h, high:high + share, :] = c_ref[1, h]
    for slot, tap in ((OWN, 2), (N1, 1), (N2, 0)):
        wl_ref[slot, :channels, :] = wt_ref[tap]
    for slot in (C1, C0):
        wl_ref[slot, :channels, :] = jnp.zeros((channels, taps), wl_ref.dtype)

    def weights_g0(slot):
        wl_ref[slot, channels:channels + share, :] = wc_ref[0]
        wl_ref[slot, high:high + share, :] = wc_ref[1]

    def weights_g1(slot):
        wl_ref[slot, high:high + share, :] = wc_ref[0]

    @pl.when(j == 0)
    def _():
        weights_g0(OWN)
        weights_g1(N1)

    pl.when(j == 1)(lambda: weights_g1(OWN))
    weights_g1(C1)
    weights_g0(C0)

    lane = lax.broadcasted_iota(jnp.int32, (channels, cols), 1)
    wide = 128
    wlane = lax.broadcasted_iota(jnp.int32, (taps, wide), 1)

    def shift_row(slot, p):
        value = gp[slot, p]
        full = value.astype(jnp.float32)
        ahead = jnp.where(lane == cols - 1, 0.0, pltpu.roll(full, cols - 1, 1))
        behind = jnp.where(lane == 0, 0.0, pltpu.roll(full, 1, 1))
        base = pl.multiple_of(p * k_row, 16)
        sc[pl.ds(base, channels), :] = ahead.astype(jnp.bfloat16)
        sc[pl.ds(pl.multiple_of(base + channels, 16), channels), :] = value
        sc[pl.ds(pl.multiple_of(base + 2 * channels, 16), channels), :] = behind.astype(jnp.bfloat16)

    def compute_row(slot, h):
        block = sc[pl.ds(pl.multiple_of(h * k_row, 16), taps), :]
        term = jnp.dot(wl_ref[slot], block, preferred_element_type=jnp.float32)
        if slot is OWN:
            dacc[h] = term
        else:
            dacc[h] += term
        wtmp[:, :stack] += lax.dot_general(
            block, xs_ref[h], (((1,), (1,)), ((), ())), preferred_element_type=jnp.float32)

    def placed_cache(block, shift_from):
        turned = pltpu.roll(block, lax.rem(j * share + 2 * wide - shift_from, wide), 1)
        inside = jnp.logical_and(wlane >= j * share, wlane < (j + 1) * share)
        return jnp.where(inside, turned, 0.0)

    def run(step, start, stop):
        def body(i, carry):
            step(i)
            return carry

        lax.fori_loop(start, stop, body, 0)

    def process(slot):
        run(functools.partial(shift_row, slot), 0, rows + 2)
        run(functools.partial(compute_row, slot), 0, rows)

    def add_x(tap):
        acc[tap, :taps, :] += jnp.where(wlane < channels, wtmp[:, :wide], 0.0)

    def add_g0():
        acc[0, :taps, :] += placed_cache(wtmp[:, :wide], channels)
        acc[1, :taps, :] += placed_cache(wtmp[:, wide:], 0)

    def add_g1():
        acc[0, :taps, :] += placed_cache(wtmp[:, wide:], 0)

    def clear():
        wtmp[...] = jnp.zeros_like(wtmp)

    def reduction(index):
        def rs_copy(k):
            to = lax.rem(s + k, ns)
            return pltpu.make_async_remote_copy(
                src_ref=sb.at[index, to], dst_ref=rb.at[index, s],
                send_sem=rs_send.at[index, k], recv_sem=rs_recv.at[index, s],
                device_id={"space": to}, device_id_type=MESH)

        def rs_landed(k):
            source = lax.rem(s + ns - k, ns)
            return pltpu.make_async_remote_copy(
                src_ref=sb.at[index, source], dst_ref=rb.at[index, source],
                send_sem=rs_send.at[index, k], recv_sem=rs_recv.at[index, source],
                device_id={"space": source}, device_id_type=MESH)

        def z_copy(k):
            return pltpu.make_async_remote_copy(
                src_ref=zs.at[index], dst_ref=zb.at[index, j],
                send_sem=zz_send.at[index, k], recv_sem=zz_recv.at[index, j],
                device_id={"tm": lax.rem(j + k, nz)}, device_id_type=MESH)

        def z_landed(k):
            source = lax.rem(j + nz - k, nz)
            return pltpu.make_async_remote_copy(
                src_ref=zs.at[index], dst_ref=zb.at[index, source],
                send_sem=zz_send.at[index, k], recv_sem=zz_recv.at[index, source],
                device_id={"tm": source}, device_id_type=MESH)

        def ag_copy(k):
            return pltpu.make_async_remote_copy(
                src_ref=gb.at[index, s], dst_ref=gb.at[index, s],
                send_sem=ag_send.at[index, k], recv_sem=ag_recv.at[index, s],
                device_id={"space": lax.rem(s + k, ns)}, device_id_type=MESH)

        def ag_landed(k):
            source = lax.rem(s + ns - k, ns)
            return pltpu.make_async_remote_copy(
                src_ref=gb.at[index, source], dst_ref=gb.at[index, source],
                send_sem=ag_send.at[index, k], recv_sem=ag_recv.at[index, source],
                device_id={"space": source}, device_id_type=MESH)

        def scatter():
            for q in range(ns):
                sb[index, q] = acc[index, q * ck:(q + 1) * ck, :].astype(jnp.bfloat16)
            for k in range(1, ns):
                rs_copy(k).start()

        def across():
            total = acc[index, pl.ds(pl.multiple_of(s * ck, 16), ck), :]
            for k in range(1, ns):
                rs_landed(k).wait_recv()
                total = total + rb[index, lax.rem(s + ns - k, ns)].astype(jnp.float32)
            zs[index] = total.astype(jnp.bfloat16)
            for k in range(1, nz):
                z_copy(k).start()

        def gather():
            zb[index, j] = zs[index]
            for k in range(1, nz):
                z_landed(k).wait_recv()
            total = zb[index, 0].astype(jnp.float32)
            for q in range(1, nz):
                total = total + zb[index, q].astype(jnp.float32)
            gb[index, s] = (total * scale).astype(jnp.bfloat16)
            for k in range(1, ns):
                ag_copy(k).start()

        def finish():
            for k in range(1, ns):
                ag_landed(k).wait_recv()
            for q in range(ns):
                acc[index, q * ck:(q + 1) * ck, :] = gb[index, q].astype(jnp.float32)
            for b in range(3):
                for d in range(3):
                    at = (b * 3 + d) * channels
                    wg_ref[index, 2 - b, d] = acc[index, at:at + channels, :channels]
            for k in range(1, ns):
                rs_copy(k).wait_send()
                ag_copy(k).wait_send()
            for k in range(1, nz):
                z_copy(k).wait_send()

        return scatter, across, gather, finish

    steps = [reduction(tap) for tap in range(3)]
    scatter, across, gather, finish = range(4)

    halo_wait(OWN)
    process(OWN)
    add_x(2)
    steps[2][scatter]()
    pl.when(j == 0)(add_g0)
    pl.when(j == 1)(add_g1)
    clear()

    has_n1 = j < last
    passes_on = j < last

    def c1_row(r):
        @pl.when(j >= 2)
        def _():
            own_c1(r).wait_recv()
            pl.when(passes_on)(lambda: fwd_c1(r).start())

    def halo_after(slot, r):
        if r == 0:
            halo_start_up(slot)
        if r == rows - 1:
            halo_start_down(slot)

    c1_row(order[0])
    for count, r in enumerate(order):
        @pl.when(j >= 1)
        def _():
            own_c0(r).wait_recv()
            pl.when(passes_on)(lambda: fwd_c0(r).start())
            halo_after(C0, r)

        @pl.when(has_n1)
        def _():
            to_prev(r).wait_recv()
            pl.when(j >= 1)(lambda: fwd_prev(r).start())
            halo_after(N1, r)

        if count == 1:
            steps[2][across]()
        if count == 2:
            steps[2][gather]()

    @pl.when(j == 1)
    def _():
        for r in order[1:]:
            own_c1(r).start()

    @pl.when(has_n1)
    def _():
        halo_wait(N1)
        process(N1)
        add_x(1)
        pl.when(j == 0)(add_g1)
        clear()

    c1_row(order[1])

    @pl.when(j >= 1)
    def _():
        halo_wait(C0)
        process(C0)
        add_g0()
        clear()

    steps[1][scatter]()
    for r in order[2:-1]:
        c1_row(r)

    def late_row(r):
        row_copy(FWD_PREV, N1, late, r, prev).wait_recv()

    for r in order[:-1]:
        @pl.when(j < last - 1)
        def _():
            late_row(r)

        halo_after(late, r)
    missing = order[-1] + 1
    halo_wait(late)
    run(functools.partial(shift_row, late), 0, missing)
    run(functools.partial(shift_row, late), missing + 1, rows + 2)
    run(functools.partial(compute_row, late), 0, missing - 2)
    steps[1][across]()
    c1_row(order[-1])

    @pl.when(j < last - 1)
    def _():
        late_row(order[-1])

    shift_row(late, missing)
    run(functools.partial(compute_row, late), missing - 2, rows)
    pl.when(j < last - 1)(lambda: add_x(0))
    pl.when(j >= last - 1)(add_g1)
    steps[0][scatter]()
    steps[1][gather]()
    for h in range(rows):
        ig_ref[h] = dacc[h, :channels, :].astype(jnp.bfloat16)
        cg_ref[0, h] = dacc[h, channels:channels + share, :].astype(jnp.bfloat16)
        cg_ref[1, h] = dacc[h, high:high + share, :].astype(jnp.bfloat16)
    steps[2][finish]()
    steps[0][across]()
    steps[1][finish]()
    steps[0][gather]()

    for r in range(rows):
        @pl.when(j >= 1)
        def _():
            to_prev(r).wait_send()

        @pl.when(jnp.logical_and(j >= 1, has_n1))
        def _():
            fwd_prev(r).wait_send()

        @pl.when(j == 0)
        def _():
            own_c0(r).wait_send()

        @pl.when(j == 1)
        def _():
            own_c1(r).wait_send()

        @pl.when(jnp.logical_and(j >= 1, passes_on))
        def _():
            fwd_c0(r).wait_send()

        @pl.when(jnp.logical_and(j >= 2, passes_on))
        def _():
            fwd_c1(r).wait_send()
    steps[0][finish]()


def up_to(value, step):
    return -(-value // step) * step


def per_device(nz, ns, frames, cache, grad_out, weight):
    j = lax.axis_index("tm")
    _, channels, rows, cols = frames.shape
    share = cache.shape[1]
    taps = 9 * channels
    stack = 128 + up_to(share, 32)
    ck = up_to(-(-taps // ns), 16)
    g = jnp.transpose(grad_out[0], (1, 0, 2))
    x = jnp.transpose(frames[0], (1, 0, 2))
    c = jnp.transpose(cache, (0, 2, 1, 3))
    wt = jnp.transpose(weight[:, ::-1], (0, 4, 1, 2, 3)).reshape(3, channels, taps)
    wc = lax.dynamic_slice_in_dim(wt[:2], j * share, share, axis=1)
    scale = 1.0 / math.sqrt(nz * ns * rows * cols)
    f32, bf16 = jnp.float32, jnp.bfloat16
    vmem = pl.BlockSpec(memory_space=pltpu.VMEM)
    dma = pltpu.SemaphoreType.DMA
    ig, cg, weight_grad = pl.pallas_call(
        functools.partial(kernel, nz, ns, ck, channels, share, scale),
        out_shape=(
            jax.ShapeDtypeStruct((rows, channels, cols), bf16),
            jax.ShapeDtypeStruct((2, rows, share, cols), bf16),
            jax.ShapeDtypeStruct(weight.shape, f32),
        ),
        in_specs=[vmem] * 5,
        out_specs=(vmem,) * 3,
        scratch_shapes=[
            pltpu.VMEM((5, rows + 2, channels, cols), bf16),
            pltpu.VMEM(((rows + 2) * 3 * channels, cols), bf16),
            pltpu.VMEM((rows, stack, cols), f32),
            pltpu.VMEM((taps, 256), f32),
            pltpu.VMEM((3, ns * ck, 128), f32),
            pltpu.VMEM((rows, stack, cols), bf16),
            pltpu.VMEM((5, stack, taps), bf16),
            pltpu.VMEM((3, ns, ck, 128), bf16), pltpu.VMEM((3, ns, ck, 128), bf16),
            pltpu.VMEM((3, ck, 128), bf16), pltpu.VMEM((3, nz, ck, 128), bf16),
            pltpu.VMEM((3, ns, ck, 128), bf16),
            dma((5, rows)), dma((5, rows)), dma((5, 2)), dma((5, 2)),
            dma((3, ns)), dma((3, ns)), dma((3, nz)), dma((3, nz)), dma((3, ns)), dma((3, ns)),
        ],
        compiler_params=pltpu.CompilerParams(
            collective_id=0, has_side_effects=True, vmem_limit_bytes=60 * 1024 * 1024),
    )(g, x, c, wt, wc)
    return (jnp.transpose(ig, (1, 0, 2))[None], jnp.transpose(cg, (0, 2, 1, 3)), weight_grad)


def solution(mesh):
    placed = (
        P("tm", None, "space", None),
        P(None, "tm", "space", None),
        P("tm", None, "space", None),
        P(),
    )
    return jax.shard_map(
        functools.partial(per_device, mesh.shape["tm"], mesh.shape["space"]),
        mesh=mesh,
        in_specs=placed,
        out_specs=(P("tm", None, "space", None), P(None, "tm", "space", None), P()),
        check_vma=False,
    )
```

```python
import functools
import math

import jax
import jax.numpy as jnp
from jax import lax
from jax.experimental import pallas as pl
from jax.experimental.pallas import tpu as pltpu
from jax.sharding import PartitionSpec as P

MESH = pl.DeviceIdType.MESH
OWN, N1, N2, C1, C0 = range(5)
TO_PREV, FWD_PREV, TO_NEXT, FWD_C1, FWD_C0 = range(5)


def kernel(
    nz, ns, ck, channels, share,
    g_ref, x_ref, c_ref, wt_ref, wc_ref, ig_ref, cg_ref, wg_ref,
    gp, sc, dacc, wtmp, acc, xs_ref, wl_ref,
    sb, rb, zs, zb, gb,
    z_send, z_recv, h_send, h_recv,
    rs_send, rs_recv, zz_send, zz_recv, ag_send, ag_recv,
):
    assert nz == 4
    j = lax.axis_index("tm")
    s = lax.axis_index("space")
    rows, _, cols = g_ref.shape
    k_row = 3 * channels
    taps = 3 * k_row
    last = nz - 1
    order = [0, rows - 1, *range(1, rows - 1)]
    high = 128
    late = jnp.where(j < last - 1, N2, C1)

    barrier = pltpu.get_barrier_semaphore()
    for k in range(1, ns):
        pl.semaphore_signal(barrier, inc=1, device_id={"space": lax.rem(s + k, ns)}, device_id_type=MESH)
    for k in range(1, nz):
        pl.semaphore_signal(barrier, inc=1, device_id={"tm": lax.rem(j + k, nz)}, device_id_type=MESH)
    pl.semaphore_wait(barrier, ns - 1 + nz - 1)

    def row_copy(stream, slot_from, slot_to, r, target):
        src = g_ref.at[r] if slot_from == OWN else gp.at[slot_from, r + 1]
        return pltpu.make_async_remote_copy(
            src_ref=src, dst_ref=gp.at[slot_to, r + 1],
            send_sem=z_send.at[stream, r], recv_sem=z_recv.at[slot_to, r],
            device_id={"tm": target}, device_id_type=MESH)

    prev = lax.rem(j + nz - 1, nz)
    nxt = lax.rem(j + 1, nz)

    def to_prev(r):
        return row_copy(TO_PREV, OWN, N1, r, prev)

    def fwd_prev(r):
        return row_copy(FWD_PREV, N1, N2, r, prev)

    def own_c0(r):
        return row_copy(TO_NEXT, OWN, C0, r, nxt)

    def own_c1(r):
        return row_copy(TO_NEXT, OWN, C1, r, nxt)

    def fwd_c1(r):
        return row_copy(FWD_C1, C1, C1, r, nxt)

    def fwd_c0(r):
        return row_copy(FWD_C0, C0, C0, r, nxt)

    for r in order:
        pl.when(j >= 1)(lambda: to_prev(r).start())
        pl.when(j == 0)(lambda: own_c0(r).start())
    pl.when(j == 1)(lambda: own_c1(order[0]).start())

    def halo_up(slot):
        src = g_ref.at[0] if slot is OWN else gp.at[slot, 1]
        return pltpu.make_async_remote_copy(
            src_ref=src, dst_ref=gp.at[slot, rows + 1],
            send_sem=h_send.at[slot, 0], recv_sem=h_recv.at[slot, 0],
            device_id={"space": lax.rem(s + ns - 1, ns)}, device_id_type=MESH)

    def halo_down(slot):
        src = g_ref.at[rows - 1] if slot is OWN else gp.at[slot, rows]
        return pltpu.make_async_remote_copy(
            src_ref=src, dst_ref=gp.at[slot, 0],
            send_sem=h_send.at[slot, 1], recv_sem=h_recv.at[slot, 1],
            device_id={"space": lax.rem(s + 1, ns)}, device_id_type=MESH)

    def halo_start_up(slot):
        pl.when(s >= 1)(lambda: halo_up(slot).start())

    def halo_start_down(slot):
        pl.when(s < ns - 1)(lambda: halo_down(slot).start())

    def halo_wait(slot):
        @pl.when(s >= 1)
        def _():
            halo_up(slot).wait_send()
            halo_down(slot).wait_recv()

        @pl.when(s < ns - 1)
        def _():
            halo_down(slot).wait_send()
            halo_up(slot).wait_recv()

    halo_start_up(OWN)
    halo_start_down(OWN)

    @pl.when(s == 0)
    def _():
        for slot in range(5):
            gp[slot, 0] = jnp.zeros(gp.shape[2:], gp.dtype)

    @pl.when(s == ns - 1)
    def _():
        for slot in range(5):
            gp[slot, rows + 1] = jnp.zeros(gp.shape[2:], gp.dtype)

    for r in range(rows):
        gp[OWN, r + 1] = g_ref[r]
    wtmp[...] = jnp.zeros_like(wtmp)
    acc[...] = jnp.zeros_like(acc)
    stack = xs_ref.shape[1]
    xs_ref[:, channels:, :] = jnp.zeros((rows, stack - channels, cols), xs_ref.dtype)
    wl_ref[:, channels:, :] = jnp.zeros((5, stack - channels, taps), wl_ref.dtype)
    for h in range(rows):
        xs_ref[h, :channels, :] = x_ref[h]
        xs_ref[h, channels:channels + share, :] = c_ref[0, h]
        xs_ref[h, high:high + share, :] = c_ref[1, h]
    for slot, tap in ((OWN, 2), (N1, 1), (N2, 0)):
        wl_ref[slot, :channels, :] = wt_ref[tap]
    for slot in (C1, C0):
        wl_ref[slot, :channels, :] = jnp.zeros((channels, taps), wl_ref.dtype)

    def weights_g0(slot):
        wl_ref[slot, channels:channels + share, :] = wc_ref[0]
        wl_ref[slot, high:high + share, :] = wc_ref[1]

    def weights_g1(slot):
        wl_ref[slot, high:high + share, :] = wc_ref[0]

    @pl.when(j == 0)
    def _():
        weights_g0(OWN)
        weights_g1(N1)

    pl.when(j == 1)(lambda: weights_g1(OWN))
    weights_g1(C1)
    weights_g0(C0)

    lane = lax.broadcasted_iota(jnp.int32, (channels, cols), 1)
    wide = 128
    wlane = lax.broadcasted_iota(jnp.int32, (taps, wide), 1)

    def shift_row(slot, p):
        value = gp[slot, p]
        full = value.astype(jnp.float32)
        ahead = jnp.where(lane == cols - 1, 0.0, pltpu.roll(full, cols - 1, 1))
        behind = jnp.where(lane == 0, 0.0, pltpu.roll(full, 1, 1))
        base = pl.multiple_of(p * k_row, 16)
        sc[pl.ds(base, channels), :] = ahead.astype(jnp.bfloat16)
        sc[pl.ds(pl.multiple_of(base + channels, 16), channels), :] = value
        sc[pl.ds(pl.multiple_of(base + 2 * channels, 16), channels), :] = behind.astype(jnp.bfloat16)

    def compute_row(slot, h):
        block = sc[pl.ds(pl.multiple_of(h * k_row, 16), taps), :]
        term = jnp.dot(wl_ref[slot], block, preferred_element_type=jnp.float32)
        if slot is OWN:
            dacc[h] = term
        else:
            dacc[h] += term
        wtmp[:, :stack] += lax.dot_general(
            block, xs_ref[h], (((1,), (1,)), ((), ())), preferred_element_type=jnp.float32)

    def placed_cache(block, shift_from):
        turned = pltpu.roll(block, lax.rem(j * share + 2 * wide - shift_from, wide), 1)
        inside = jnp.logical_and(wlane >= j * share, wlane < (j + 1) * share)
        return jnp.where(inside, turned, 0.0)

    def run(step, start, stop):
        def body(i, carry):
            step(i)
            return carry

        lax.fori_loop(start, stop, body, 0)

    def process(slot):
        run(functools.partial(shift_row, slot), 0, rows + 2)
        run(functools.partial(compute_row, slot), 0, rows)

    def add_x(tap):
        acc[tap, :taps, :] += jnp.where(wlane < channels, wtmp[:, :wide], 0.0)

    def add_g0():
        acc[0, :taps, :] += placed_cache(wtmp[:, :wide], channels)
        acc[1, :taps, :] += placed_cache(wtmp[:, wide:], 0)

    def add_g1():
        acc[0, :taps, :] += placed_cache(wtmp[:, wide:], 0)

    def clear():
        wtmp[...] = jnp.zeros_like(wtmp)

    def reduction(index):
        def rs_copy(k):
            to = lax.rem(s + k, ns)
            return pltpu.make_async_remote_copy(
                src_ref=sb.at[index, to], dst_ref=rb.at[index, s],
                send_sem=rs_send.at[index, k], recv_sem=rs_recv.at[index, s],
                device_id={"space": to}, device_id_type=MESH)

        def rs_landed(k):
            source = lax.rem(s + ns - k, ns)
            return pltpu.make_async_remote_copy(
                src_ref=sb.at[index, source], dst_ref=rb.at[index, source],
                send_sem=rs_send.at[index, k], recv_sem=rs_recv.at[index, source],
                device_id={"space": source}, device_id_type=MESH)

        def z_copy(k):
            return pltpu.make_async_remote_copy(
                src_ref=zs.at[index], dst_ref=zb.at[index, j],
                send_sem=zz_send.at[index, k], recv_sem=zz_recv.at[index, j],
                device_id={"tm": lax.rem(j + k, nz)}, device_id_type=MESH)

        def z_landed(k):
            source = lax.rem(j + nz - k, nz)
            return pltpu.make_async_remote_copy(
                src_ref=zs.at[index], dst_ref=zb.at[index, source],
                send_sem=zz_send.at[index, k], recv_sem=zz_recv.at[index, source],
                device_id={"tm": source}, device_id_type=MESH)

        def ag_copy(k):
            return pltpu.make_async_remote_copy(
                src_ref=gb.at[index, s], dst_ref=gb.at[index, s],
                send_sem=ag_send.at[index, k], recv_sem=ag_recv.at[index, s],
                device_id={"space": lax.rem(s + k, ns)}, device_id_type=MESH)

        def ag_landed(k):
            source = lax.rem(s + ns - k, ns)
            return pltpu.make_async_remote_copy(
                src_ref=gb.at[index, source], dst_ref=gb.at[index, source],
                send_sem=ag_send.at[index, k], recv_sem=ag_recv.at[index, source],
                device_id={"space": source}, device_id_type=MESH)

        def scatter():
            for q in range(ns):
                sb[index, q] = acc[index, q * ck:(q + 1) * ck, :].astype(jnp.bfloat16)
            for k in range(1, ns):
                rs_copy(k).start()

        def across():
            total = acc[index, pl.ds(pl.multiple_of(s * ck, 16), ck), :]
            for k in range(1, ns):
                rs_landed(k).wait_recv()
                total = total + rb[index, lax.rem(s + ns - k, ns)].astype(jnp.float32)
            zs[index] = total.astype(jnp.bfloat16)
            for k in range(1, nz):
                z_copy(k).start()

        def gather():
            zb[index, j] = zs[index]
            for k in range(1, nz):
                z_landed(k).wait_recv()
            total = zb[index, 0].astype(jnp.float32)
            for q in range(1, nz):
                total = total + zb[index, q].astype(jnp.float32)
            gb[index, s] = total.astype(jnp.bfloat16)
            for k in range(1, ns):
                ag_copy(k).start()

        def finish():
            for k in range(1, ns):
                ag_landed(k).wait_recv()
            for q in range(ns):
                acc[index, q * ck:(q + 1) * ck, :] = gb[index, q].astype(jnp.float32)
            for b in range(3):
                for d in range(3):
                    at = (b * 3 + d) * channels
                    wg_ref[index, 2 - b, d] = acc[index, at:at + channels, :channels]
            for k in range(1, ns):
                rs_copy(k).wait_send()
                ag_copy(k).wait_send()
            for k in range(1, nz):
                z_copy(k).wait_send()

        return scatter, across, gather, finish

    steps = [reduction(tap) for tap in range(3)]
    scatter, across, gather, finish = range(4)

    has_n1 = j < last
    passes_on = j < last

    def c1_row(r):
        @pl.when(j >= 2)
        def _():
            own_c1(r).wait_recv()
            pl.when(passes_on)(lambda: fwd_c1(r).start())

    def halo_after(slot, r):
        if r == 0:
            halo_start_up(slot)
        if r == rows - 1:
            halo_start_down(slot)

    def c0_row(r):
        own_c0(r).wait_recv()
        pl.when(passes_on)(lambda: fwd_c0(r).start())
        halo_after(C0, r)

    c1_row(order[0])
    pl.when(j == 1)(lambda: c0_row(order[0]))
    halo_wait(OWN)
    process(OWN)
    add_x(2)
    steps[2][scatter]()
    pl.when(j == 0)(add_g0)
    pl.when(j == 1)(add_g1)
    clear()

    for count, r in enumerate(order):
        pl.when(j >= (2 if count == 0 else 1))(lambda: c0_row(r))

        @pl.when(has_n1)
        def _():
            to_prev(r).wait_recv()
            pl.when(j >= 1)(lambda: fwd_prev(r).start())
            halo_after(N1, r)


    @pl.when(j == 1)
    def _():
        for r in order[1:]:
            own_c1(r).start()

    @pl.when(has_n1)
    def _():
        halo_wait(N1)
        process(N1)
        add_x(1)
        pl.when(j == 0)(add_g1)
        clear()

    c1_row(order[1])

    @pl.when(j >= 1)
    def _():
        halo_wait(C0)
        process(C0)
        add_g0()
        clear()

    steps[1][scatter]()
    for r in order[2:-1]:
        c1_row(r)

    def late_row(r):
        row_copy(FWD_PREV, N1, late, r, prev).wait_recv()

    for r in order[:-1]:
        @pl.when(j < last - 1)
        def _():
            late_row(r)

        halo_after(late, r)
    missing = order[-1] + 1
    halo_wait(late)
    run(functools.partial(shift_row, late), 0, missing)
    run(functools.partial(shift_row, late), missing + 1, rows + 2)
    run(functools.partial(compute_row, late), 0, missing - 2)
    c1_row(order[-1])
    steps[2][across]()
    steps[1][across]()

    @pl.when(j < last - 1)
    def _():
        late_row(order[-1])

    shift_row(late, missing)
    run(functools.partial(compute_row, late), missing - 2, rows)
    pl.when(j < last - 1)(lambda: add_x(0))
    pl.when(j >= last - 1)(add_g1)
    steps[0][scatter]()
    steps[2][gather]()
    steps[1][gather]()
    for h in range(rows):
        ig_ref[h] = dacc[h, :channels, :].astype(jnp.bfloat16)
        cg_ref[0, h] = dacc[h, channels:channels + share, :].astype(jnp.bfloat16)
        cg_ref[1, h] = dacc[h, high:high + share, :].astype(jnp.bfloat16)
    steps[0][across]()
    steps[2][finish]()
    steps[1][finish]()
    steps[0][gather]()

    for r in range(rows):
        @pl.when(j >= 1)
        def _():
            to_prev(r).wait_send()

        @pl.when(jnp.logical_and(j >= 1, has_n1))
        def _():
            fwd_prev(r).wait_send()

        @pl.when(j == 0)
        def _():
            own_c0(r).wait_send()

        @pl.when(j == 1)
        def _():
            own_c1(r).wait_send()

        @pl.when(jnp.logical_and(j >= 1, passes_on))
        def _():
            fwd_c0(r).wait_send()

        @pl.when(jnp.logical_and(j >= 2, passes_on))
        def _():
            fwd_c1(r).wait_send()
    steps[0][finish]()


def up_to(value, step):
    return -(-value // step) * step


def per_device(nz, ns, frames, cache, grad_out, weight):
    j = lax.axis_index("tm")
    _, channels, rows, cols = frames.shape
    share = cache.shape[1]
    taps = 9 * channels
    stack = 128 + up_to(share, 32)
    ck = up_to(-(-taps // ns), 16)
    g = jnp.transpose(grad_out[0], (1, 0, 2))
    x = jnp.transpose(frames[0], (1, 0, 2))
    c = jnp.transpose(cache, (0, 2, 1, 3))
    wt = jnp.transpose(weight[:, ::-1], (0, 4, 1, 2, 3)).reshape(3, channels, taps)
    wc = lax.dynamic_slice_in_dim(wt[:2], j * share, share, axis=1)
    scale = 1.0 / math.sqrt(nz * ns * rows * cols)
    f32, bf16 = jnp.float32, jnp.bfloat16
    vmem = pl.BlockSpec(memory_space=pltpu.VMEM)
    dma = pltpu.SemaphoreType.DMA
    ig, cg, weight_grad = pl.pallas_call(
        functools.partial(kernel, nz, ns, ck, channels, share),
        out_shape=(
            jax.ShapeDtypeStruct((rows, channels, cols), bf16),
            jax.ShapeDtypeStruct((2, rows, share, cols), bf16),
            jax.ShapeDtypeStruct(weight.shape, f32),
        ),
        in_specs=[vmem] * 5,
        out_specs=(vmem,) * 3,
        scratch_shapes=[
            pltpu.VMEM((5, rows + 2, channels, cols), bf16),
            pltpu.VMEM(((rows + 2) * 3 * channels, cols), bf16),
            pltpu.VMEM((rows, stack, cols), f32),
            pltpu.VMEM((taps, 256), f32),
            pltpu.VMEM((3, ns * ck, 128), f32),
            pltpu.VMEM((rows, stack, cols), bf16),
            pltpu.VMEM((5, stack, taps), bf16),
            pltpu.VMEM((3, ns, ck, 128), bf16), pltpu.VMEM((3, ns, ck, 128), bf16),
            pltpu.VMEM((3, ck, 128), bf16), pltpu.VMEM((3, nz, ck, 128), bf16),
            pltpu.VMEM((3, ns, ck, 128), bf16),
            dma((5, rows)), dma((5, rows)), dma((5, 2)), dma((5, 2)),
            dma((3, ns)), dma((3, ns)), dma((3, nz)), dma((3, nz)), dma((3, ns)), dma((3, ns)),
        ],
        compiler_params=pltpu.CompilerParams(
            collective_id=0, has_side_effects=True, vmem_limit_bytes=60 * 1024 * 1024),
    )(g, x, c, wt, wc)
    return (jnp.transpose(ig, (1, 0, 2))[None], jnp.transpose(cg, (0, 2, 1, 3)), weight_grad * scale)


def solution(mesh):
    placed = (
        P("tm", None, "space", None),
        P(None, "tm", "space", None),
        P("tm", None, "space", None),
        P(),
    )
    return jax.shard_map(
        functools.partial(per_device, mesh.shape["tm"], mesh.shape["space"]),
        mesh=mesh,
        in_specs=placed,
        out_specs=(P("tm", None, "space", None), P(None, "tm", "space", None), P()),
        check_vma=False,
    )
```
